128 devices in a mesh: level: 8 (over z, y_hi), leaf: 8 (over x, core), rhs: 2 (over y_lo).
Axes of the slice: x: 4, y: 4 (y_hi: 2, y_lo: 2; y = y_hi * 2 + y_lo), z: 4, core: 2. Of those that a mesh axis runs over, the one named last changes fastest.
Arguments:
- charges: float32 [64, 262144], P(None, ('level', 'leaf', 'rhs')), may hold values from -6 to 6
- cluster_order: int32 [262144], P(('level', 'leaf')), may hold values from 0 to 4095, as said below
- near_tiles: float32 [2048, 4, 128, 128], P(('level', 'leaf', 'rhs')), may hold values from -0.25 to 0.25
- near_index: int32 [2048, 4], P(('level', 'leaf', 'rhs')), may hold values from 0 to 31, as said below
- near_count: int32 [2048], P(('level', 'leaf', 'rhs')), may hold values from 1 to 4, as said below
- proj_basis: float32 [4, 262144, 256], P(None, ('level', 'leaf', 'rhs'))
- corr_basis: float32 [4, 256, 262144], P(None, None, ('level', 'leaf', 'rhs')), may hold values from -0.1875 to 0.1875
- coupling: float32 [64, 4, 2, 256, 256], P(('level', 'leaf'))
Outputs:
- solution: float32 [64, 262144], P(None, ('level', 'leaf', 'rhs'))
The draws below stay inside these ranges and needn't reach their ends.
Inputs may be any that keep to these rules, and one draw needn't show every extreme that they name: `cluster_order`: every aligned block of 4096 entries is a permutation of 0 to 4095. `near_index`: the entries of a row are distinct tile numbers of the same leaf, the first being the row's own tile. `near_count`: the first tile row of every leaf has 4.
All inputs are finite; a program needn't handle non-finite values.
Results may differ from the reference program's by a relative error of at most 0.0001.
Values sent between devices are 32-bit elements; how exact they have to be, the bound alone decides.
No kernel may reach another device: no remote copies, remote signals or barrier semaphores. Data moves between devices by JAX's collectives and lax.ppermute only.
A program may use at most 128 MiB of HBM per device.

```python
import jax
import jax.numpy as jnp
from jax import lax

RANK = 256
NRHS = 64
TILE = 128
NEAR = 4
LEVELS = 4
LEAF = 4096
NPTS = 262144


def draw_cluster_order(key, part):
    leaves = NPTS // LEAF
    keys = jax.random.split(key, leaves)
    perms = jax.vmap(lambda single: jax.random.permutation(single, LEAF))(keys)
    return perms.reshape(NPTS).astype(jnp.int32)


def draw_near_index(key, part):
    tiles_leaf = LEAF // TILE
    row_total = NPTS // TILE
    keys = jax.random.split(jax.random.fold_in(key, 11), row_total)
    shifts = jax.vmap(lambda single: jax.random.permutation(single, tiles_leaf - 1)[:NEAR - 1] + 1)(keys)
    own_tile = jnp.arange(row_total, dtype=jnp.int32) % tiles_leaf
    offsets = jnp.concatenate([jnp.zeros((row_total, 1), jnp.int32), shifts.astype(jnp.int32)], axis=1)
    return ((own_tile[:, None] + offsets) % tiles_leaf).astype(jnp.int32)


def draw_near_count(key, part):
    tiles_leaf = LEAF // TILE
    row_total = NPTS // TILE
    counts = jax.random.randint(jax.random.fold_in(key, 23), (row_total,), 1, NEAR + 1).astype(jnp.int32)
    first_row = jnp.arange(row_total, dtype=jnp.int32) % tiles_leaf == 0
    return jnp.where(first_row, NEAR, counts).astype(jnp.int32)


def draw_proj_basis(key, part):
    heights = jnp.arange(LEVELS, dtype=jnp.float32)
    scales = (LEAF * 2.0 ** heights) ** (-0.5)
    values = jax.random.normal(key, (LEVELS, NPTS, RANK), jnp.float32)
    return values * scales[:, None, None]


def draw_coupling(key, part):
    leaves = NPTS // LEAF
    shape = (LEVELS, leaves // 2, 2, RANK, 2, RANK)
    noise = jax.random.normal(key, shape, jnp.float32)
    noise = noise * (0.4 / (2.0 * RANK) ** 0.5)
    leaf_ids = jnp.arange(leaves, dtype=jnp.int32)
    eye_block = jnp.eye(RANK, dtype=jnp.float32)
    stacked = []
    for height in range(LEVELS):
        nodes = leaf_ids // 2 ** (height + 1)
        child_bit = leaf_ids // 2 ** height % 2
        blocks = noise[height][nodes]
        first = (child_bit == 0)[:, None, None]
        own_block = jnp.where(first, blocks[:, 1, :, 0, :], blocks[:, 0, :, 1, :])
        sib_block = jnp.where(first, blocks[:, 1, :, 1, :], blocks[:, 0, :, 0, :]) + eye_block[None]
        stacked.append(jnp.stack([own_block, sib_block], axis=1))
    return jnp.stack(stacked, axis=1)


def level_of(key, dims, shards, low, largest):
    factor_of, own = 1.0, jax.random.fold_in(key, 6)
    for position, parts in shards:
        steps = jnp.exp(jax.random.uniform(jax.random.fold_in(own, position), (parts,), jnp.float32, low / len(shards), largest / len(shards)))
        factor_of = factor_of * jnp.repeat(steps, dims[position] // parts).reshape([-1 if axis == position else 1 for axis in range(len(dims))])
    return factor_of


def bell_draw(stream_key, shape, scale, bound, pieces=(), kind=jnp.bfloat16):
    factor_of = level_of(stream_key, shape, pieces, -0.22, 0.18) if pieces else 1.0
    result = jax.random.normal(stream_key, shape, jnp.float32) * scale * factor_of
    return jnp.minimum(jnp.maximum(result, -bound), bound).astype(kind)


def setup_inputs(seed: int = 0) -> dict:
    splits = jax.random.split(jax.random.key(seed), 9)
    charges = bell_draw(splits[0], (NRHS, NPTS), 1.0, 6.0, ((1, 128),), jnp.float32)
    cluster_order = draw_cluster_order(jax.random.fold_in(splits[8], 71), 0)
    near_tiles = bell_draw(splits[2], (NPTS // TILE, NEAR, TILE, TILE), (NEAR * TILE) ** -0.5, 0.25, ((0, 128),), jnp.float32)
    near_index = draw_near_index(jax.random.fold_in(splits[8], 71), 0)
    near_count = draw_near_count(jax.random.fold_in(splits[8], 71), 0)
    proj_basis = draw_proj_basis(jax.random.fold_in(splits[8], 71), 0)
    corr_basis = bell_draw(splits[6], (LEVELS, RANK, NPTS), (4 * RANK) ** -0.5, 0.1875, ((2, 128),), jnp.float32)
    coupling = draw_coupling(jax.random.fold_in(splits[8], 71), 0)
    return {"charges": charges, "cluster_order": cluster_order, "near_tiles": near_tiles, "near_index": near_index, "near_count": near_count, "proj_basis": proj_basis, "corr_basis": corr_basis, "coupling": coupling}


def reference(charges, cluster_order, near_tiles, near_index, near_count, proj_basis, corr_basis, coupling):
    leaves = NPTS // LEAF
    tiles_leaf = LEAF // TILE
    by_leaf = charges.reshape(NRHS, leaves, LEAF)
    local_order = cluster_order.reshape(leaves, LEAF)
    ordered = jnp.take_along_axis(by_leaf, local_order[None, :, :], axis=2)
    blocks = ordered.reshape(NRHS, leaves, tiles_leaf, TILE)
    index = near_index.reshape(leaves, tiles_leaf, NEAR)

    def pick_tiles(leaf_blocks, leaf_index):
        return leaf_blocks[:, leaf_index]

    picked = jax.vmap(pick_tiles, in_axes=(1, 0), out_axes=1)(blocks, index)
    live_mask = (jnp.arange(NEAR)[None, :] < near_count[:, None]).astype(jnp.float32)
    live_mask = live_mask.reshape(leaves, tiles_leaf, NEAR)
    picked = picked * live_mask[None, :, :, :, None]
    tiles = near_tiles.reshape(leaves, tiles_leaf, NEAR, TILE, TILE)
    current = jnp.einsum("rltki,ltkio->rlto", picked, tiles, precision=lax.Precision.HIGHEST)
    current = current.reshape(NRHS, leaves, LEAF)
    for height in range(LEVELS):
        span = 2 ** height
        basis = proj_basis[height].reshape(leaves, LEAF, RANK)
        projected = jnp.einsum("rln,lnk->rlk", current, basis, precision=lax.Precision.HIGHEST)
        own_sum = projected.reshape(NRHS, leaves // span, span, RANK).sum(axis=2)
        sib_sum = jnp.flip(own_sum.reshape(NRHS, leaves // (2 * span), 2, RANK), axis=2)
        sib_sum = sib_sum.reshape(NRHS, leaves // span, RANK)
        own_rows = jnp.repeat(own_sum, span, axis=1)
        sib_rows = jnp.repeat(sib_sum, span, axis=1)
        coeff = jnp.einsum("rlk,lkj->rlj", own_rows, coupling[:, height, 0], precision=lax.Precision.HIGHEST)
        coeff = coeff + jnp.einsum("rlk,lkj->rlj", sib_rows, coupling[:, height, 1], precision=lax.Precision.HIGHEST)
        correction = corr_basis[height].reshape(RANK, leaves, LEAF)
        current = current - jnp.einsum("rlk,kln->rln", coeff, correction, precision=lax.Precision.HIGHEST)
    return current.reshape(NRHS, NPTS)
```

```python
import jax
import jax.numpy as jnp
from jax import lax
from jax.sharding import PartitionSpec as P


def from_partner(block, axis, distance):
    count = lax.axis_size(axis)
    route = []
    for low in range(count):
        high = low | 1 << distance
        if high != low and high < count:
            route += [(low, high), (high, low)]
    return lax.ppermute(block, axis, route)


def partner_sum(values, bit_pos):
    return from_partner(values, ("level", "leaf"), bit_pos)


def local(
    charges, cluster_order, near_tiles, near_index, near_count, proj_basis, corr_basis, coupling
):
    rhs_count = charges.shape[0]
    row_count = charges.shape[1]
    near_slots = near_tiles.shape[1]
    tile_size = near_tiles.shape[2]
    other = from_partner(charges, "rhs", 0)
    first = lax.axis_index("rhs") == 0
    leaf_charges = jnp.concatenate(
        [jnp.where(first, charges, other), jnp.where(first, other, charges)], axis=1
    )
    ordered = jnp.take(leaf_charges, cluster_order, axis=1)
    blocks = ordered.reshape(rhs_count, -1, tile_size)
    picked = blocks[:, near_index]
    live_mask = (jnp.arange(near_slots)[None, :] < near_count[:, None]).astype(jnp.float32)
    picked = picked * live_mask[None, :, :, None]
    current = jnp.einsum("rtki,tkio->rto", picked, near_tiles, precision=lax.Precision.HIGH)
    current = current.reshape(rhs_count, row_count)
    for height in range(proj_basis.shape[0]):
        projected = jnp.dot(
            current,
            proj_basis[height],
            precision=lax.Precision.HIGH,
            preferred_element_type=jnp.float32,
        )
        own_sum = projected + from_partner(projected, "rhs", 0)
        for bit_pos in range(height):
            own_sum = own_sum + partner_sum(own_sum, bit_pos)
        sib_sum = partner_sum(own_sum, height)
        coeff = jnp.dot(
            own_sum,
            coupling[0, height, 0],
            precision=lax.Precision.HIGH,
            preferred_element_type=jnp.float32,
        )
        coeff = coeff + jnp.dot(
            sib_sum,
            coupling[0, height, 1],
            precision=lax.Precision.HIGH,
            preferred_element_type=jnp.float32,
        )
        current = current - jnp.dot(
            coeff,
            corr_basis[height],
            precision=lax.Precision.HIGH,
            preferred_element_type=jnp.float32,
        )
    return current


def solution(mesh):
    return jax.shard_map(
        local,
        mesh=mesh,
        in_specs=(
            P(None, ("level", "leaf", "rhs")),
            P(("level", "leaf")),
            P(("level", "leaf", "rhs"), None, None, None),
            P(("level", "leaf", "rhs"), None),
            P(("level", "leaf", "rhs")),
            P(None, ("level", "leaf", "rhs"), None),
            P(None, None, ("level", "leaf", "rhs")),
            P(("level", "leaf"), None, None, None, None),
        ),
        out_specs=P(None, ("level", "leaf", "rhs")),
        check_vma=False,
    )
```

```python
import jax
import jax.numpy as jnp
from jax import lax
from jax.sharding import Mesh, PartitionSpec as P

AXES = ("z", "y", "x1", "x0", "core", "rhs")
FAST = lax.Precision.HIGH


def dot(a, b):
    return jnp.dot(a, b, precision=FAST, preferred_element_type=jnp.float32)


def swap(block, axes, mask):
    count = lax.axis_size(axes)
    return lax.ppermute(block, axes, [(i, i ^ mask) for i in range(count)])


def over_rhs(block):
    return swap(block, ("rhs",), 1)


PARTNERS = (
    (("core",), 1),
    (("x0",), 1),
    (("x1", "x0"), 3),
    (("y", "x1", "x0", "core", "rhs"), 17),
)


def local(
    charges, cluster_order, near_tiles, near_index, near_count, proj_basis, corr_basis, coupling
):
    rhs_count = charges.shape[0]
    row_count = charges.shape[1]
    near_slots = near_tiles.shape[1]
    tile_size = near_tiles.shape[2]
    levels = proj_basis.shape[0]
    other = over_rhs(charges)
    gram = {}
    for low in range(levels):
        for high in range(low + 1, levels):
            gram[low, high] = dot(corr_basis[low], proj_basis[high])
    first = lax.axis_index("rhs") == 0
    leaf_charges = jnp.concatenate(
        [jnp.where(first, charges, other), jnp.where(first, other, charges)], axis=1
    )
    ordered = jnp.take(leaf_charges, cluster_order, axis=1)
    blocks = ordered.reshape(rhs_count, -1, tile_size)
    picked = blocks[:, near_index]
    live_mask = (jnp.arange(near_slots)[None, :] < near_count[:, None]).astype(jnp.float32)
    picked = picked * live_mask[None, :, :, None]
    current = jnp.einsum("rtki,tkio->rto", picked, near_tiles, precision=FAST)
    current = current.reshape(rhs_count, row_count)
    reduced = [dot(current, proj_basis[height]) for height in range(levels)]
    for height in range(levels):
        own_sum = reduced[height]
        own_sum = own_sum + over_rhs(own_sum)
        for axes, mask in PARTNERS[:height]:
            own_sum = own_sum + swap(own_sum, axes, mask)
        sib_sum = swap(own_sum, *PARTNERS[height])
        coeff = dot(own_sum, coupling[0, height, 0]) + dot(sib_sum, coupling[0, height, 1])
        for high in range(height + 1, levels):
            reduced[high] = reduced[high] - dot(coeff, gram[height, high])
        current = current - dot(coeff, corr_basis[height])
    return current


def solution(mesh):
    split = Mesh(mesh.devices.reshape(-1, 2, 2, 2, 2, 2), AXES)
    every = AXES
    leaf = AXES[:-1]
    return jax.shard_map(
        local,
        mesh=split,
        in_specs=(
            P(None, every),
            P(leaf),
            P(every, None, None, None),
            P(every, None),
            P(every),
            P(None, every, None),
            P(None, None, every),
            P(leaf, None, None, None, None),
        ),
        out_specs=P(None, every),
        check_vma=False,
    )
```

```python
import jax
import jax.numpy as jnp
from jax import lax
from jax.experimental import pallas as pl
from jax.experimental.pallas import tpu as pltpu
from jax.sharding import Mesh, PartitionSpec as P

AXES = ("z", "y", "x1", "x0", "core", "rhs")
FAST = lax.Precision.HIGH


def dot(a, b):
    return jnp.dot(a, b, precision=FAST, preferred_element_type=jnp.float32)


def swap(block, axes, mask):
    count = lax.axis_size(axes)
    return lax.ppermute(block, axes, [(i, i ^ mask) for i in range(count)])


def over_rhs(block):
    return swap(block, ("rhs",), 1)


RING = ("y", "x1", "x0", "core", "rhs")


def mm(a, b):
    return jnp.dot(a, b, preferred_element_type=jnp.float32)

def parts(value):
    high = value.astype(jnp.bfloat16)
    low = (value - high.astype(jnp.float32)).astype(jnp.bfloat16)
    return high, low

def stacked(value):
    high, low = parts(value)
    return jnp.concatenate([high, low], axis=0)

def near_kernel(order, index, count, side, own, other, tiles_hbm, proj_hbm, current, reduced,
                source, gathered, operand, tiles, proj, needed, tile_sem, proj_sem):
    rows, half = own.shape
    size = tiles.shape[-1]
    slots = index.shape[1]
    leaf_tiles = operand.shape[0]
    out_tiles = tiles.shape[0]
    load_tiles = pltpu.make_async_copy(tiles_hbm, tiles, tile_sem)
    load_tiles.start()
    load_proj = pltpu.make_async_copy(proj_hbm.at[0], proj, proj_sem)
    load_proj.start()
    own_start = side[0] * half
    other_start = half - own_start
    for block, start in ((own, own_start), (other, other_start)):
        for c in range(half // size):
            at = pl.multiple_of(start + c * size, size)
            source[pl.ds(at, size), :] = block[:, c * size:(c + 1) * size].T

    for tile in range(leaf_tiles):
        needed[tile] = 0
    def mark(t, _):
        for slot in range(slots):
            @pl.when(slot < count[t])
            def _():
                needed[index[t, slot]] = 1
        return 0
    lax.fori_loop(0, out_tiles, mark, 0)

    def gather(tile, _):
        @pl.when(needed[tile] == 1)
        def _():
            def rows_of(step, _):
                base = tile * size + step * 16
                for u in range(16):
                    gathered[pl.ds(step * 16 + u, 1), :] = source[pl.ds(order[base + u], 1), :]
                return 0
            lax.fori_loop(0, size // 16, rows_of, 0)
            operand[tile] = stacked(gathered[...].T)
        return 0
    lax.fori_loop(0, leaf_tiles, gather, 0)

    load_tiles.wait()
    def near(t, _):
        pieces = []
        for slot in range(slots):
            live = slot < count[t]
            picked = operand[jnp.where(live, index[t, slot], index[t, 0])]
            pieces.append(jnp.where(live, picked, jnp.zeros_like(picked)))
        left = jnp.concatenate(pieces, axis=1)
        high, low = parts(tiles[t].reshape(slots * size, size))
        both = mm(left, high)
        out = both[:rows] + both[rows:] + mm(left[:rows], low)
        current[:, pl.ds(pl.multiple_of(t * size, size), size)] = out
        return 0
    lax.fori_loop(0, out_tiles, near, 0, unroll=4)
    load_proj.wait()
    total = jnp.zeros(reduced.shape, jnp.float32)
    for c in range(half // 256):
        left = stacked(current[:, c * 256:(c + 1) * 256])
        high, low = parts(proj[c * 256:(c + 1) * 256, :])
        both = mm(left, high)
        total = total + (both[:rows] + both[rows:] + mm(left[:rows], low))
    reduced[...] = total

def near_call(order, index, count, side, own, other, tiles, proj):
    rows, half = own.shape
    out_tiles, slots, size, _ = tiles.shape
    rank = proj.shape[-1]
    smem = pl.BlockSpec(memory_space=pltpu.SMEM)
    vmem = pl.BlockSpec(memory_space=pltpu.VMEM)
    hbm = pl.BlockSpec(memory_space=pl.ANY)
    return pl.pallas_call(
        near_kernel,
        out_shape=(jax.ShapeDtypeStruct((rows, half), jnp.float32), jax.ShapeDtypeStruct((rows, rank), jnp.float32)),
        in_specs=[smem, smem, smem, smem, vmem, vmem, hbm, hbm],
        out_specs=(vmem, vmem),
        scratch_shapes=[
            pltpu.VMEM((order.shape[0], rows), jnp.float32),
            pltpu.VMEM((size, rows), jnp.float32),
            pltpu.VMEM((order.shape[0] // size, 2 * rows, size), jnp.bfloat16),
            pltpu.VMEM(tiles.shape, jnp.float32),
            pltpu.VMEM((half, rank), jnp.float32),
            pltpu.SMEM((order.shape[0] // size,), jnp.int32),
            pltpu.SemaphoreType.DMA,
            pltpu.SemaphoreType.DMA,
        ],
        compiler_params=pltpu.CompilerParams(vmem_limit_bytes=54 << 20),
        cost_estimate=pl.CostEstimate(flops=200_000_000, bytes_accessed=8 << 20, transcendentals=0),
        name="near",
    )(order, index, count, side, own, other, tiles, proj)

def gram_kernel(corr_hbm, proj_hbm, *rest):
    levels, points, rank = proj_hbm.shape
    pairs = levels * (levels - 1) // 2
    grams = rest[:pairs]
    corr, proj, sems = rest[pairs:]
    loads = {}
    for level in range(levels - 1):
        loads["c", level] = pltpu.make_async_copy(corr_hbm.at[level], corr.at[level], sems.at[level])
        loads["p", level] = pltpu.make_async_copy(
            proj_hbm.at[level + 1], proj.at[level], sems.at[levels - 1 + level])
        loads["c", level].start()
        loads["p", level].start()
    lefts = []
    for above in range(levels - 1):
        loads["c", above].wait()
        left_high, left_low = parts(corr[above])
        lefts.append((left_high, left_low))
        loads["p", above].wait()
        high, low = parts(proj[above])
        for below in range(above + 1):
            left_high, left_low = lefts[below]
            grams[above * (above + 1) // 2 + below][...] = (
                mm(left_high, high) + mm(left_high, low) + mm(left_low, high))

def gram_call(corr, proj):
    levels, points, rank = proj.shape
    pairs = levels * (levels - 1) // 2
    hbm = pl.BlockSpec(memory_space=pl.ANY)
    vmem = pl.BlockSpec(memory_space=pltpu.VMEM)
    return pl.pallas_call(
        gram_kernel,
        out_shape=[jax.ShapeDtypeStruct((rank, rank), jnp.float32)] * pairs,
        in_specs=[hbm, hbm],
        out_specs=[vmem] * pairs,
        scratch_shapes=[
            pltpu.VMEM((levels - 1, rank, points), jnp.float32),
            pltpu.VMEM((levels - 1, points, rank), jnp.float32),
            pltpu.SemaphoreType.DMA((2 * levels - 2,)),
        ],
        compiler_params=pltpu.CompilerParams(vmem_limit_bytes=54 << 20),
        cost_estimate=pl.CostEstimate(
            flops=6 * pairs * points * rank * rank, bytes_accessed=12 << 20, transcendentals=0),
        name="gram",
    )(corr, proj)


def local(
    charges, cluster_order, near_tiles, near_index, near_count, proj_basis, corr_basis, coupling
):
    levels = proj_basis.shape[0]
    other = over_rhs(charges)
    grams = gram_call(corr_basis, proj_basis)
    other, grams = lax.optimization_barrier((other, grams))
    side = lax.axis_index("rhs").astype(jnp.int32).reshape(1)
    current, first = near_call(
        cluster_order, near_index, near_count, side, charges, other, near_tiles, proj_basis
    )
    reduced = [first] + [dot(current, proj_basis[height]) for height in range(1, levels)]
    for height in range(levels):
        own_sum = reduced[height]
        if height < 3:
            own_sum = own_sum + over_rhs(own_sum)
        if height > 0:
            own_sum = own_sum + swap(own_sum, ("core",), 1)
        if height == 0:
            sib_sum = swap(own_sum, ("core",), 1)
        elif height == 1:
            sib_sum = swap(own_sum, ("x0",), 1)
        else:
            near, far, across = (swap(own_sum, ("x1", "x0"), mask) for mask in (1, 3, 2))
            own_sum = own_sum + near
            sib_sum = far + across
        if height == 3:
            own_sum = own_sum + sib_sum
            near, far, across = (swap(own_sum, RING, mask) for mask in (1, 17, 16))
            own_sum = own_sum + near
            sib_sum = far + across
        coeff = dot(own_sum, coupling[0, height, 0]) + dot(sib_sum, coupling[0, height, 1])
        for high in range(height + 1, levels):
            pair = high * (high - 1) // 2 + height
            reduced[high] = reduced[high] - dot(coeff, grams[pair])
        current = current - dot(coeff, corr_basis[height])
    return current


def solution(mesh):
    split = Mesh(mesh.devices.reshape(-1, 2, 2, 2, 2, 2), AXES)
    every = AXES
    leaf = AXES[:-1]
    return jax.shard_map(
        local,
        mesh=split,
        in_specs=(
            P(None, every),
            P(leaf),
            P(every, None, None, None),
            P(every, None),
            P(every),
            P(None, every, None),
            P(None, None, every),
            P(leaf, None, None, None, None),
        ),
        out_specs=P(None, every),
        check_vma=False,
    )
```

```python
import jax
import jax.numpy as jnp
from jax import lax
from jax.experimental import pallas as pl
from jax.experimental.pallas import tpu as pltpu
from jax.sharding import Mesh, PartitionSpec as P

AXES = ("z", "y", "x1", "x0", "core", "rhs")
FAST = lax.Precision.HIGH


def dot(a, b):
    return jnp.dot(a, b, precision=FAST, preferred_element_type=jnp.float32)


def swap(block, axes, mask):
    count = lax.axis_size(axes)
    return lax.ppermute(block, axes, [(i, i ^ mask) for i in range(count)])


def over_rhs(block):
    return swap(block, ("rhs",), 1)


RING = ("y", "x1", "x0", "core", "rhs")


def mm(a, b):
    return jnp.dot(a, b, preferred_element_type=jnp.float32)

def parts(value):
    high = value.astype(jnp.bfloat16)
    low = (value - high.astype(jnp.float32)).astype(jnp.bfloat16)
    return high, low

def stacked(value):
    high, low = parts(value)
    return jnp.concatenate([high, low], axis=0)

def near_kernel(order, index, count, side, own, other, tiles_hbm, proj_hbm, current, reduced,
                source, gathered, operand, tiles, proj, needed, wanted, tile_sem, proj_sem):
    rows, half = own.shape
    size = tiles.shape[-1]
    slots = index.shape[1]
    leaf_tiles = operand.shape[0]
    out_tiles = tiles.shape[0]
    load_tiles = pltpu.make_async_copy(tiles_hbm, tiles, tile_sem)
    load_tiles.start()
    load_proj = pltpu.make_async_copy(proj_hbm.at[pl.ds(0, 2)], proj, proj_sem)
    load_proj.start()
    own_start = side[0] * half
    other_start = half - own_start
    for block, start in ((own, own_start), (other, other_start)):
        for c in range(half // size):
            at = pl.multiple_of(start + c * size, size)
            source[pl.ds(at, size), :] = block[:, c * size:(c + 1) * size].T

    for tile in range(leaf_tiles):
        needed[tile] = 0
    for t in range(out_tiles):
        for slot in range(slots):
            needed[index[t, jnp.where(slot < count[t], slot, 0)]] = 1

    def note(tile, found):
        wanted[found] = tile
        return found + needed[tile]
    found = lax.fori_loop(0, leaf_tiles, note, 0, unroll=True)
    wanted[found] = wanted[found - 1]

    def fetch(base, slot):
        for u in range(size):
            gathered[slot, pl.ds(u, 1), :] = source[pl.ds(order[base + u], 1), :]

    fetch(wanted[0] * size, 0)
    def gather(n, _):
        slot = n & 1
        ready = stacked(gathered[slot].T)
        fetch(wanted[n + 1] * size, 1 - slot)
        operand[wanted[n]] = ready
        return 0
    lax.fori_loop(0, found, gather, 0)

    load_tiles.wait()
    def near(t, _):
        pieces = []
        for slot in range(slots):
            live = slot < count[t]
            picked = operand[jnp.where(live, index[t, slot], index[t, 0])]
            pieces.append(jnp.where(live, picked, jnp.zeros_like(picked)))
        left = jnp.concatenate(pieces, axis=1)
        high, low = parts(tiles[t].reshape(slots * size, size))
        both = mm(left, high)
        out = both[:rows] + both[rows:] + mm(left[:rows], low)
        current[:, pl.ds(pl.multiple_of(t * size, size), size)] = out
        return 0
    lax.fori_loop(0, out_tiles, near, 0, unroll=8)
    load_proj.wait()
    left = stacked(current[...])
    for level in range(2):
        high, low = parts(proj[level])
        both = mm(left, high)
        reduced[level * rows:(level + 1) * rows, :] = (
            both[:rows] + both[rows:] + mm(left[:rows], low))

def near_call(order, index, count, side, own, other, tiles, proj):
    rows, half = own.shape
    out_tiles, slots, size, _ = tiles.shape
    rank = proj.shape[-1]
    smem = pl.BlockSpec(memory_space=pltpu.SMEM)
    vmem = pl.BlockSpec(memory_space=pltpu.VMEM)
    hbm = pl.BlockSpec(memory_space=pltpu.HBM)
    return pl.pallas_call(
        near_kernel,
        out_shape=(jax.ShapeDtypeStruct((rows, half), jnp.float32), jax.ShapeDtypeStruct((2 * rows, rank), jnp.float32)),
        in_specs=[smem, smem, smem, smem, vmem, vmem, hbm, hbm],
        out_specs=(vmem, vmem),
        scratch_shapes=[
            pltpu.VMEM((order.shape[0], rows), jnp.float32),
            pltpu.VMEM((2, size, rows), jnp.float32),
            pltpu.VMEM((order.shape[0] // size, 2 * rows, size), jnp.bfloat16),
            pltpu.VMEM(tiles.shape, jnp.float32),
            pltpu.VMEM((2, half, rank), jnp.float32),
            pltpu.SMEM((order.shape[0] // size,), jnp.int32),
            pltpu.SMEM((order.shape[0] // size + 1,), jnp.int32),
            pltpu.SemaphoreType.DMA,
            pltpu.SemaphoreType.DMA,
        ],
        compiler_params=pltpu.CompilerParams(vmem_limit_bytes=48 << 20),
        cost_estimate=pl.CostEstimate(flops=200_000_000, bytes_accessed=8 << 20, transcendentals=0),
        name="near",
    )(order, index, count, side, own, other,
      *(pltpu.with_memory_space_constraint(v, pltpu.HBM) for v in (tiles, proj)))

def gram_kernel(corr_hbm, proj_hbm, *rest):
    levels, points, rank = proj_hbm.shape
    early, second, mid, late, corr, proj, sems = rest
    targets = {(0, 0): (early, 0), (1, 0): (second, 0), (1, 1): (mid, 0),
               (2, 0): (late, 0), (2, 1): (late, 1), (2, 2): (late, 2)}
    loads = {}
    for level in range(levels - 1):
        loads["c", level] = pltpu.make_async_copy(corr_hbm.at[level], corr.at[level], sems.at[level])
        loads["p", level] = pltpu.make_async_copy(
            proj_hbm.at[level + 1], proj.at[level], sems.at[levels - 1 + level])
        loads["c", level].start()
        loads["p", level].start()
    lefts = []
    for above in range(levels - 1):
        loads["c", above].wait()
        left_high, left_low = parts(corr[above])
        lefts.append((left_high, left_low))
        loads["p", above].wait()
        high, low = parts(proj[above])
        for below in range(above + 1):
            left_high, left_low = lefts[below]
            target, place = targets[above, below]
            target[place * rank:(place + 1) * rank, :] = (
                mm(left_high, high) + mm(left_high, low) + mm(left_low, high))

def gram_call(corr, proj):
    levels, points, rank = proj.shape
    pairs = levels * (levels - 1) // 2
    hbm = pl.BlockSpec(memory_space=pltpu.HBM)
    vmem = pl.BlockSpec(memory_space=pltpu.VMEM)
    return pl.pallas_call(
        gram_kernel,
        out_shape=[jax.ShapeDtypeStruct((above * rank, rank), jnp.float32) for above in (1, 1, 1, 3)],
        in_specs=[hbm, hbm],
        out_specs=[vmem] * levels,
        scratch_shapes=[
            pltpu.VMEM((levels - 1, rank, points), jnp.float32),
            pltpu.VMEM((levels - 1, points, rank), jnp.float32),
            pltpu.SemaphoreType.DMA((2 * levels - 2,)),
        ],
        compiler_params=pltpu.CompilerParams(vmem_limit_bytes=54 << 20),
        cost_estimate=pl.CostEstimate(
            flops=6 * pairs * points * rank * rank, bytes_accessed=12 << 20, transcendentals=0),
        name="gram",
    )(*(pltpu.with_memory_space_constraint(v, pltpu.HBM) for v in (corr, proj)))


def local(
    charges, cluster_order, near_tiles, near_index, near_count, proj_basis, corr_basis, coupling
):
    tie = lax.optimization_barrier
    rank = proj_basis.shape[-1]
    other = over_rhs(charges)
    early, second, mid, late = gram_call(corr_basis, proj_basis)
    early_other = over_rhs(early)
    second_other = over_rhs(second)
    other, early, second, mid, late = tie((other, early, second, mid, late))
    side = lax.axis_index("rhs").astype(jnp.int32).reshape(1)
    current, pair = near_call(
        cluster_order, near_index, near_count, side, charges, other, near_tiles, proj_basis
    )
    pair, early_other = tie((pair, early_other))
    early = early + early_other
    pair = pair + over_rhs(pair)
    own, sum1 = pair[:charges.shape[0]], pair[charges.shape[0]:]
    own, mid, second_other = tie((own, mid, second_other))
    second = second + second_other
    mid = mid + over_rhs(mid)
    part2 = dot(current, proj_basis[2])
    sum2 = part2 + over_rhs(part2)
    part3 = dot(current, proj_basis[3])

    def coefficients(height, own, sib):
        return dot(own, coupling[0, height, 0]) + dot(sib, coupling[0, height, 1])

    coeff0 = coefficients(0, own, swap(own, ("core",), 1))
    own = sum1 - dot(coeff0, early)
    own = own + swap(own, ("core",), 1)
    current = current - dot(coeff0, corr_basis[0])
    sum2 = sum2 - dot(coeff0, second)
    part3 = part3 - dot(coeff0, late[:rank])
    coeff1 = coefficients(1, own, swap(own, ("x0",), 1))
    own = sum2 - dot(coeff1, mid)
    own = own + swap(own, ("core",), 1)
    current = current - dot(coeff1, corr_basis[1])
    part3 = part3 - dot(coeff1, late[rank:2 * rank])
    near, far, across = (swap(own, ("x1", "x0"), mask) for mask in (1, 3, 2))
    coeff2 = coefficients(2, own + near, far + across)
    own = part3 - dot(coeff2, late[2 * rank:])
    own = own + swap(own, ("core",), 1)
    current = current - dot(coeff2, corr_basis[2])
    near, far, across = (swap(own, ("x1", "x0"), mask) for mask in (1, 3, 2))
    own = (own + near) + (far + across)
    near, far, across = (swap(own, RING, mask) for mask in (1, 17, 16))
    coeff3 = coefficients(3, own + near, far + across)
    return current - dot(coeff3, corr_basis[3])


def solution(mesh):
    split = Mesh(mesh.devices.reshape(-1, 2, 2, 2, 2, 2), AXES)
    every = AXES
    leaf = AXES[:-1]
    return jax.shard_map(
        local,
        mesh=split,
        in_specs=(
            P(None, every),
            P(leaf),
            P(every, None, None, None),
            P(every, None),
            P(every),
            P(None, every, None),
            P(None, None, every),
            P(leaf, None, None, None, None),
        ),
        out_specs=P(None, every),
        check_vma=False,
    )
```

```python
import jax
import jax.numpy as jnp
from jax import lax
from jax.experimental import pallas as pl
from jax.experimental.pallas import tpu as pltpu
from jax.sharding import Mesh, PartitionSpec as P

AXES = ("z", "y", "x1", "x0", "core", "rhs")
FAST = lax.Precision.HIGH


def dot(a, b):
    return jnp.dot(a, b, precision=FAST, preferred_element_type=jnp.float32)


def swap(block, axes, mask):
    count = lax.axis_size(axes)
    return lax.ppermute(block, axes, [(i, i ^ mask) for i in range(count)])


def over_rhs(block):
    return swap(block, ("rhs",), 1)


RING = ("y", "x1", "x0", "core", "rhs")


def mm(a, b):
    return jnp.dot(a, b, preferred_element_type=jnp.float32)

def parts(value):
    high = value.astype(jnp.bfloat16)
    low = (value - high.astype(jnp.float32)).astype(jnp.bfloat16)
    return high, low

def stacked(value):
    high, low = parts(value)
    return jnp.concatenate([high, low], axis=0)

def near_kernel(order, index, count, side, own, other, tiles_hbm, proj_hbm, current, reduced,
                source, gathered, operand, tiles, proj, needed, wanted, tile_sem, proj_sem):
    rows, half = own.shape
    size = tiles.shape[-1]
    slots = index.shape[1]
    leaf_tiles = operand.shape[0]
    out_tiles = tiles.shape[0]
    load_tiles = pltpu.make_async_copy(tiles_hbm, tiles, tile_sem)
    load_tiles.start()
    load_proj = pltpu.make_async_copy(proj_hbm.at[pl.ds(0, 2)], proj, proj_sem)
    load_proj.start()
    own_start = side[0] * half
    other_start = half - own_start
    for block, start in ((own, own_start), (other, other_start)):
        for c in range(half // size):
            at = pl.multiple_of(start + c * size, size)
            source[pl.ds(at, size), :] = block[:, c * size:(c + 1) * size].T

    for tile in range(leaf_tiles):
        needed[tile] = 0
    for t in range(out_tiles):
        for slot in range(slots):
            needed[index[t, jnp.where(slot < count[t], slot, 0)]] = 1

    def note(tile, found):
        wanted[found] = tile
        return found + needed[tile]
    found = lax.fori_loop(0, leaf_tiles, note, 0, unroll=True)
    wanted[found] = wanted[found - 1]

    def fetch(base, slot):
        for u in range(size):
            gathered[slot, pl.ds(u, 1), :] = source[pl.ds(order[base + u], 1), :]

    fetch(wanted[0] * size, 0)
    def gather(n, _):
        slot = n & 1
        ready = stacked(gathered[slot].T)
        fetch(wanted[n + 1] * size, 1 - slot)
        operand[wanted[n]] = ready
        return 0
    lax.fori_loop(0, found, gather, 0)

    load_tiles.wait()
    def near(t, _):
        pieces = []
        for slot in range(slots):
            live = slot < count[t]
            picked = operand[jnp.where(live, index[t, slot], index[t, 0])]
            pieces.append(jnp.where(live, picked, jnp.zeros_like(picked)))
        left = jnp.concatenate(pieces, axis=1)
        high, low = parts(tiles[t].reshape(slots * size, size))
        both = mm(left, high)
        out = both[:rows] + both[rows:] + mm(left[:rows], low)
        current[:, pl.ds(pl.multiple_of(t * size, size), size)] = out
        return 0
    lax.fori_loop(0, out_tiles, near, 0, unroll=8)
    load_proj.wait()
    left = stacked(current[...])
    for level in range(2):
        high, low = parts(proj[level])
        both = mm(left, high)
        reduced[level * rows:(level + 1) * rows, :] = (
            both[:rows] + both[rows:] + mm(left[:rows], low))

def near_call(order, index, count, side, own, other, tiles, proj):
    rows, half = own.shape
    out_tiles, slots, size, _ = tiles.shape
    rank = proj.shape[-1]
    smem = pl.BlockSpec(memory_space=pltpu.SMEM)
    vmem = pl.BlockSpec(memory_space=pltpu.VMEM)
    hbm = pl.BlockSpec(memory_space=pltpu.HBM)
    return pl.pallas_call(
        near_kernel,
        out_shape=(jax.ShapeDtypeStruct((rows, half), jnp.float32), jax.ShapeDtypeStruct((2 * rows, rank), jnp.float32)),
        in_specs=[smem, smem, smem, smem, vmem, vmem, hbm, hbm],
        out_specs=(vmem, vmem),
        scratch_shapes=[
            pltpu.VMEM((order.shape[0], rows), jnp.float32),
            pltpu.VMEM((2, size, rows), jnp.float32),
            pltpu.VMEM((order.shape[0] // size, 2 * rows, size), jnp.bfloat16),
            pltpu.VMEM(tiles.shape, jnp.float32),
            pltpu.VMEM((2, half, rank), jnp.float32),
            pltpu.SMEM((order.shape[0] // size,), jnp.int32),
            pltpu.SMEM((order.shape[0] // size + 1,), jnp.int32),
            pltpu.SemaphoreType.DMA,
            pltpu.SemaphoreType.DMA,
        ],
        compiler_params=pltpu.CompilerParams(vmem_limit_bytes=24 << 20),
        cost_estimate=pl.CostEstimate(flops=200_000_000, bytes_accessed=8 << 20, transcendentals=0),
        name="near",
    )(order, index, count, side, own, other,
      *(pltpu.with_memory_space_constraint(v, pltpu.HBM) for v in (tiles, proj)))

def later_kernel(current, proj_hbm, reduced, proj, sems):
    rows = current.shape[0]
    loads = [pltpu.make_async_copy(proj_hbm.at[level + 2], proj.at[level], sems.at[level])
             for level in range(2)]
    for load in loads:
        load.start()
    left = stacked(current[...])
    for level in range(2):
        loads[level].wait()
        high, low = parts(proj[level])
        both = mm(left, high)
        reduced[level * rows:(level + 1) * rows, :] = (
            both[:rows] + both[rows:] + mm(left[:rows], low))


def later_call(current, proj):
    rows, points = current.shape
    rank = proj.shape[-1]
    vmem = pl.BlockSpec(memory_space=pltpu.VMEM)
    return pl.pallas_call(
        later_kernel,
        out_shape=jax.ShapeDtypeStruct((2 * rows, rank), jnp.float32),
        in_specs=[vmem, pl.BlockSpec(memory_space=pltpu.HBM)],
        out_specs=vmem,
        scratch_shapes=[pltpu.VMEM((2, points, rank), jnp.float32), pltpu.SemaphoreType.DMA((2,))],
        compiler_params=pltpu.CompilerParams(vmem_limit_bytes=16 << 20),
        cost_estimate=pl.CostEstimate(
            flops=12 * rows * points * rank, bytes_accessed=4 << 20, transcendentals=0),
        name="later",
    )(current, pltpu.with_memory_space_constraint(proj, pltpu.HBM))


def gram_kernel(corr_hbm, proj_hbm, coup_hbm, *rest):
    levels, points, rank = proj_hbm.shape
    early, second, mid, late, fold, corr, proj, coup, sems, coup_sem = rest
    load_coup = pltpu.make_async_copy(coup_hbm.at[0, levels - 2], coup, coup_sem)
    load_coup.start()
    loads = {}
    for level in range(levels - 1):
        loads["c", level] = pltpu.make_async_copy(corr_hbm.at[level], corr.at[level], sems.at[level])
        loads["p", level] = pltpu.make_async_copy(
            proj_hbm.at[level + 1], proj.at[level], sems.at[levels - 1 + level])
        loads["c", level].start()
        loads["p", level].start()
    targets = {(0, 0): (early, 0), (1, 0): (second, 0), (1, 1): (mid, 0),
               (2, 0): (late, 0), (2, 1): (late, 1), (2, 2): (late, 2)}
    lefts = []
    for above in range(levels - 1):
        loads["c", above].wait()
        left_high, left_low = parts(corr[above])
        lefts.append((left_high, left_low))
        loads["p", above].wait()
        high, low = parts(proj[above])
        for below in range(above + 1):
            left_high, left_low = lefts[below]
            target, place = targets[above, below]
            target[place * rank:(place + 1) * rank, :] = (
                mm(left_high, high) + mm(left_high, low) + mm(left_low, high))
    load_coup.wait()
    left_high, left_low = parts(coup[...].reshape(2 * rank, rank))
    high, low = parts(late[2 * rank:3 * rank, :])
    out = mm(left_high, high) + mm(left_high, low) + mm(left_low, high)
    for part in range(2):
        fold[part] = out[:, part * rank // 2:(part + 1) * rank // 2]


def gram_call(corr, proj, coup):
    levels, points, rank = proj.shape
    pairs = levels * (levels - 1) // 2
    hbm = pl.BlockSpec(memory_space=pltpu.HBM)
    vmem = pl.BlockSpec(memory_space=pltpu.VMEM)
    return pl.pallas_call(
        gram_kernel,
        out_shape=[jax.ShapeDtypeStruct((above * rank, rank), jnp.float32) for above in (1, 1, 1, 3)]
        + [jax.ShapeDtypeStruct((2, 2 * rank, rank // 2), jnp.float32)],
        in_specs=[hbm, hbm, hbm],
        out_specs=[vmem] * (levels + 1),
        scratch_shapes=[
            pltpu.VMEM((levels - 1, rank, points), jnp.float32),
            pltpu.VMEM((levels - 1, points, rank), jnp.float32),
            pltpu.VMEM((2, rank, rank), jnp.float32),
            pltpu.SemaphoreType.DMA((2 * levels - 2,)),
            pltpu.SemaphoreType.DMA,
        ],
        compiler_params=pltpu.CompilerParams(vmem_limit_bytes=32 << 20),
        cost_estimate=pl.CostEstimate(
            flops=6 * pairs * points * rank * rank, bytes_accessed=12 << 20, transcendentals=0),
        name="gram",
    )(*(pltpu.with_memory_space_constraint(v, pltpu.HBM) for v in (corr, proj, coup)))


def local(
    charges, cluster_order, near_tiles, near_index, near_count, proj_basis, corr_basis, coupling
):
    tie = lax.optimization_barrier
    rank = proj_basis.shape[-1]
    other = over_rhs(charges)
    early, second, mid, late, fold = gram_call(corr_basis, proj_basis, coupling)
    early_other = over_rhs(early)
    other, early, second, mid, late, fold = tie((other, early, second, mid, late, fold))
    side = lax.axis_index("rhs").astype(jnp.int32).reshape(1)
    rows = charges.shape[0]
    core = lax.axis_index("core") == 0

    def swapped(value):
        return jnp.concatenate([value[rank:], value[:rank]], axis=0)

    fold = jnp.where(core, fold[0], fold[1]) + swap(jnp.where(core, fold[1], fold[0]), ("core",), 1)
    fold_other = swap(fold, ("x0",), 1)
    current, pair = near_call(
        cluster_order, near_index, near_count, side, charges, other, near_tiles, proj_basis
    )
    pair, early_other, fold_other = tie((pair, early_other, fold_other))
    early = early + early_other
    fold = fold + fold_other
    pair = pair + over_rhs(pair)
    own, sum1 = pair[:rows], pair[rows:]
    later = later_call(current, proj_basis)
    own, later = tie((own, later))
    part2, part3 = later[:rows], later[rows:]

    def coefficients(height, own, sib):
        return dot(own, coupling[0, height, 0]) + dot(sib, coupling[0, height, 1])

    coeff0 = coefficients(0, own, swap(own, ("core",), 1))
    own = sum1 - dot(coeff0, early)
    own = own + swap(own, ("core",), 1)
    own, fold = tie((own, fold))
    fold = fold + swapped(swap(fold, ("x1", "x0"), 3))
    part2 = part2 - dot(coeff0, second)
    part3 = part3 - dot(coeff0, late[:rank])
    coeff1 = coefficients(1, own, swap(own, ("x0",), 1))
    own = part2 - dot(coeff1, mid)
    own = own + over_rhs(own)
    part3 = part3 - dot(coeff1, late[rank:2 * rank])
    both = jnp.concatenate([own, part3], axis=0)
    both = both + swap(both, ("core",), 1)
    both, fold, coeff0, coeff1 = tie((both, fold, coeff0, coeff1))
    fold_other = swap(fold, ("core",), 1)
    fold = jnp.concatenate(
        [jnp.where(core, fold, fold_other), jnp.where(core, fold_other, fold)], axis=1)
    current = current - dot(
        jnp.concatenate([coeff0, coeff1], axis=1), corr_basis[:2].reshape(2 * rank, -1))
    near, far, across = (swap(both, ("x1", "x0"), mask) for mask in (1, 3, 2))
    near = both + near
    far = far + across
    own, sib = near[:rows], far[:rows]
    coeff2 = coefficients(2, own, sib)
    own = (near[rows:] + far[rows:]) - (dot(own, fold[:rank]) + dot(sib, fold[rank:]))
    near, far, across = (swap(own, RING, mask) for mask in (1, 17, 16))
    current = current - dot(coeff2, corr_basis[2])
    coeff3 = coefficients(3, own + near, far + across)
    return current - dot(coeff3, corr_basis[3])


def solution(mesh):
    split = Mesh(mesh.devices.reshape(-1, 2, 2, 2, 2, 2), AXES)
    every = AXES
    leaf = AXES[:-1]
    return jax.shard_map(
        local,
        mesh=split,
        in_specs=(
            P(None, every),
            P(leaf),
            P(every, None, None, None),
            P(every, None),
            P(every),
            P(None, every, None),
            P(None, None, every),
            P(leaf, None, None, None, None),
        ),
        out_specs=P(None, every),
        check_vma=False,
    )
```

```python
import jax
import jax.numpy as jnp
from jax import lax
from jax.experimental import pallas as pl
from jax.experimental.pallas import tpu as pltpu
from jax.sharding import Mesh, PartitionSpec as P

AXES = ("z", "y", "x1", "x0", "core", "rhs")
FAST = lax.Precision.HIGH


def dot(a, b):
    return jnp.dot(a, b, precision=FAST, preferred_element_type=jnp.float32)


def swap(block, axes, mask):
    count = lax.axis_size(axes)
    return lax.ppermute(block, axes, [(i, i ^ mask) for i in range(count)])


def over_rhs(block):
    return swap(block, ("rhs",), 1)


RING = ("y", "x1", "x0", "core", "rhs")


def mm(a, b):
    return jnp.dot(a, b, preferred_element_type=jnp.float32)

def parts(value):
    high = value.astype(jnp.bfloat16)
    low = (value - high.astype(jnp.float32)).astype(jnp.bfloat16)
    return high, low

def stacked(value):
    high, low = parts(value)
    return jnp.concatenate([high, low], axis=0)

def near_kernel(order, index, count, side, own, other, tiles_hbm, proj_hbm, current, reduced,
                source, gathered, operand, tiles, proj, needed, wanted, tile_sem, proj_sem):
    rows, half = own.shape
    size = tiles.shape[-1]
    slots = index.shape[1]
    leaf_tiles = operand.shape[0]
    out_tiles = tiles.shape[0]
    load_tiles = pltpu.make_async_copy(tiles_hbm, tiles, tile_sem)
    load_tiles.start()
    load_proj = pltpu.make_async_copy(proj_hbm.at[pl.ds(0, 2)], proj, proj_sem)
    load_proj.start()
    own_start = side[0] * half
    other_start = half - own_start
    for block, start in ((own, own_start), (other, other_start)):
        for c in range(half // size):
            at = pl.multiple_of(start + c * size, size)
            source[pl.ds(at, size), :] = block[:, c * size:(c + 1) * size].T

    for tile in range(leaf_tiles):
        needed[tile] = 0
    for t in range(out_tiles):
        for slot in range(slots):
            needed[index[t, jnp.where(slot < count[t], slot, 0)]] = 1

    def note(tile, found):
        wanted[found] = tile
        return found + needed[tile]
    found = lax.fori_loop(0, leaf_tiles, note, 0, unroll=True)
    wanted[found] = wanted[found - 1]

    def fetch(base, slot):
        for u in range(0, size, 8):
            gathered[slot, u:u + 8, :] = jnp.concatenate(
                [source[pl.ds(order[base + u + v], 1), :] for v in range(8)], axis=0)

    fetch(wanted[0] * size, 0)
    def gather(n, _):
        slot = n & 1
        ready = stacked(gathered[slot].T)
        fetch(wanted[n + 1] * size, 1 - slot)
        operand[wanted[n]] = ready
        return 0
    lax.fori_loop(0, found, gather, 0)

    load_tiles.wait()
    def near(t, _):
        pieces = []
        for slot in range(slots):
            live = slot < count[t]
            picked = operand[jnp.where(live, index[t, slot], index[t, 0])]
            pieces.append(jnp.where(live, picked, jnp.zeros_like(picked)))
        left = jnp.concatenate(pieces, axis=1)
        high, low = parts(tiles[t].reshape(slots * size, size))
        both = mm(left, high)
        out = both[:rows] + both[rows:] + mm(left[:rows], low)
        current[:, pl.ds(pl.multiple_of(t * size, size), size)] = out
        return 0
    lax.fori_loop(0, out_tiles, near, 0, unroll=True)
    load_proj.wait()
    left = stacked(current[...])
    for level in range(2):
        high, low = parts(proj[level])
        both = mm(left, high)
        reduced[level * rows:(level + 1) * rows, :] = (
            both[:rows] + both[rows:] + mm(left[:rows], low))

def near_call(order, index, count, side, own, other, tiles, proj):
    rows, half = own.shape
    out_tiles, slots, size, _ = tiles.shape
    rank = proj.shape[-1]
    smem = pl.BlockSpec(memory_space=pltpu.SMEM)
    vmem = pl.BlockSpec(memory_space=pltpu.VMEM)
    hbm = pl.BlockSpec(memory_space=pltpu.HBM)
    return pl.pallas_call(
        near_kernel,
        out_shape=(jax.ShapeDtypeStruct((rows, half), jnp.float32), jax.ShapeDtypeStruct((2 * rows, rank), jnp.float32)),
        in_specs=[smem, smem, smem, smem, vmem, vmem, hbm, hbm],
        out_specs=(vmem, vmem),
        scratch_shapes=[
            pltpu.VMEM((order.shape[0], rows), jnp.float32),
            pltpu.VMEM((2, size, rows), jnp.float32),
            pltpu.VMEM((order.shape[0] // size, 2 * rows, size), jnp.bfloat16),
            pltpu.VMEM(tiles.shape, jnp.float32),
            pltpu.VMEM((2, half, rank), jnp.float32),
            pltpu.SMEM((order.shape[0] // size,), jnp.int32),
            pltpu.SMEM((order.shape[0] // size + 1,), jnp.int32),
            pltpu.SemaphoreType.DMA,
            pltpu.SemaphoreType.DMA,
        ],
        compiler_params=pltpu.CompilerParams(vmem_limit_bytes=24 << 20),
        cost_estimate=pl.CostEstimate(flops=200_000_000, bytes_accessed=8 << 20, transcendentals=0),
        name="near",
    )(order, index, count, side, own, other,
      *(pltpu.with_memory_space_constraint(v, pltpu.HBM) for v in (tiles, proj)))

def later_kernel(current, proj_hbm, reduced, proj, sems):
    rows = current.shape[0]
    loads = [pltpu.make_async_copy(proj_hbm.at[level + 2], proj.at[level], sems.at[level])
             for level in range(2)]
    for load in loads:
        load.start()
    left = stacked(current[...])
    for level in range(2):
        loads[level].wait()
        high, low = parts(proj[level])
        both = mm(left, high)
        reduced[level * rows:(level + 1) * rows, :] = (
            both[:rows] + both[rows:] + mm(left[:rows], low))


def later_call(current, proj):
    rows, points = current.shape
    rank = proj.shape[-1]
    vmem = pl.BlockSpec(memory_space=pltpu.VMEM)
    return pl.pallas_call(
        later_kernel,
        out_shape=jax.ShapeDtypeStruct((2 * rows, rank), jnp.float32),
        in_specs=[vmem, pl.BlockSpec(memory_space=pltpu.HBM)],
        out_specs=vmem,
        scratch_shapes=[pltpu.VMEM((2, points, rank), jnp.float32), pltpu.SemaphoreType.DMA((2,))],
        compiler_params=pltpu.CompilerParams(vmem_limit_bytes=16 << 20),
        cost_estimate=pl.CostEstimate(
            flops=12 * rows * points * rank, bytes_accessed=4 << 20, transcendentals=0),
        name="later",
    )(current, pltpu.with_memory_space_constraint(proj, pltpu.HBM))


def gram_kernel(corr_hbm, proj_hbm, coup_hbm, *rest):
    levels, points, rank = proj_hbm.shape
    early, second, mid, late, fold, corr, proj, coup, sems, coup_sem = rest
    load_coup = pltpu.make_async_copy(coup_hbm.at[0, levels - 2], coup, coup_sem)
    load_coup.start()
    loads = {}
    for level in range(levels - 1):
        loads["c", level] = pltpu.make_async_copy(corr_hbm.at[level], corr.at[level], sems.at[level])
        loads["p", level] = pltpu.make_async_copy(
            proj_hbm.at[level + 1], proj.at[level], sems.at[levels - 1 + level])
        loads["c", level].start()
        loads["p", level].start()
    targets = {(0, 0): (early, 0), (1, 0): (second, 0), (1, 1): (mid, 0),
               (2, 0): (late, 0), (2, 1): (late, 1), (2, 2): (late, 2)}
    lefts = []
    for above in range(levels - 1):
        loads["c", above].wait()
        left_high, left_low = parts(corr[above])
        lefts.append((left_high, left_low))
        loads["p", above].wait()
        high, low = parts(proj[above])
        for below in range(above + 1):
            left_high, left_low = lefts[below]
            target, place = targets[above, below]
            target[place * rank:(place + 1) * rank, :] = (
                mm(left_high, high) + mm(left_high, low) + mm(left_low, high))
    load_coup.wait()
    left_high, left_low = parts(coup[...].reshape(2 * rank, rank))
    high, low = parts(late[2 * rank:3 * rank, :])
    out = mm(left_high, high) + mm(left_high, low) + mm(left_low, high)
    for part in range(2):
        fold[part] = out[:, part * rank // 2:(part + 1) * rank // 2]


def gram_call(corr, proj, coup):
    levels, points, rank = proj.shape
    pairs = levels * (levels - 1) // 2
    hbm = pl.BlockSpec(memory_space=pltpu.HBM)
    vmem = pl.BlockSpec(memory_space=pltpu.VMEM)
    return pl.pallas_call(
        gram_kernel,
        out_shape=[jax.ShapeDtypeStruct((above * rank, rank), jnp.float32) for above in (1, 1, 1, 3)]
        + [jax.ShapeDtypeStruct((2, 2 * rank, rank // 2), jnp.float32)],
        in_specs=[hbm, hbm, hbm],
        out_specs=[vmem] * (levels + 1),
        scratch_shapes=[
            pltpu.VMEM((levels - 1, rank, points), jnp.float32),
            pltpu.VMEM((levels - 1, points, rank), jnp.float32),
            pltpu.VMEM((2, rank, rank), jnp.float32),
            pltpu.SemaphoreType.DMA((2 * levels - 2,)),
            pltpu.SemaphoreType.DMA,
        ],
        compiler_params=pltpu.CompilerParams(vmem_limit_bytes=32 << 20),
        cost_estimate=pl.CostEstimate(
            flops=6 * pairs * points * rank * rank, bytes_accessed=12 << 20, transcendentals=0),
        name="gram",
    )(*(pltpu.with_memory_space_constraint(v, pltpu.HBM) for v in (corr, proj, coup)))


def apply(value, matrix):
    rows = value.shape[0]
    left = stacked(value)
    high, low = parts(matrix)
    both = mm(left, high)
    return both[:rows] + both[rows:] + mm(left[:rows], low)


def level_coefficients(height, own, sib, coupling):
    rank = own.shape[1]
    pair = jnp.concatenate([own, sib], axis=1)
    return apply(pair, coupling[0, height].reshape(2 * rank, rank))


def first_kernel(own, sib, total, coupling, gram, coeff, after):
    value = level_coefficients(0, own[...], sib[...], coupling)
    coeff[...] = value
    after[...] = total[...] - apply(value, gram[...])


def second_kernel(own, sib, part2, part3, coupling, gram2, gram3, coeff, after2, after3):
    rank = own.shape[1]
    value = level_coefficients(1, own[...], sib[...], coupling)
    coeff[...] = value
    after2[...] = part2[...] - apply(value, gram2[...])
    after3[...] = part3[...] - apply(value, gram3[rank:2 * rank, :])


def third_kernel(both, near, far, across, fold, coupling, coeff, after):
    rows, rank = coeff.shape
    mine = both[...] + near[...]
    others = far[...] + across[...]
    own, sib = mine[:rows], others[:rows]
    coeff[...] = level_coefficients(2, own, sib, coupling)
    after[...] = (mine[rows:] + others[rows:]) - apply(
        jnp.concatenate([own, sib], axis=1), fold[...])


def middle_kernel(current, coeff, corr_hbm, after, last_high, last_low, corr, sems):
    loads = [pltpu.make_async_copy(corr_hbm.at[level + 2], corr.at[level], sems.at[level])
             for level in range(2)]
    for load in loads:
        load.start()
    loads[0].wait()
    after[...] = current[...] - apply(coeff[...], corr[0])
    loads[1].wait()
    last_high[...], last_low[...] = parts(corr[1])


def final_kernel(part, near, far, across, coupling, current, last_high, last_low, out_hbm, out, sems):
    rows, points = current.shape
    coeff = level_coefficients(3, part[...] + near[...], far[...] + across[...], coupling)
    left = stacked(coeff)
    step = points // 4
    copies = []
    for piece in range(4):
        cols = slice(piece * step, (piece + 1) * step)
        value = mm(left, last_high[:, cols])
        out[:, cols] = current[:, cols] - (
            value[:rows] + value[rows:] + mm(left[:rows], last_low[:, cols]))
        copies.append(pltpu.make_async_copy(out.at[:, cols], out_hbm.at[:, cols], sems.at[piece]))
        copies[-1].start()
    for copy in copies:
        copy.wait()


def small_call(kernel, shapes, *args):
    vmem = pl.BlockSpec(memory_space=pltpu.VMEM)
    return pl.pallas_call(
        kernel,
        out_shape=[jax.ShapeDtypeStruct(shape, jnp.float32) for shape in shapes],
        in_specs=[vmem] * len(args),
        out_specs=[vmem] * len(shapes),
        compiler_params=pltpu.CompilerParams(vmem_limit_bytes=8 << 20),
        cost_estimate=pl.CostEstimate(flops=100_000_000, bytes_accessed=1 << 20, transcendentals=0),
    )(*args)


def middle_call(current, coeff, corr):
    rank, points = corr.shape[1:]
    vmem = pl.BlockSpec(memory_space=pltpu.VMEM)
    half = jax.ShapeDtypeStruct((rank, points), jnp.bfloat16)
    return pl.pallas_call(
        middle_kernel,
        out_shape=[jax.ShapeDtypeStruct(current.shape, jnp.float32), half, half],
        in_specs=[vmem, vmem, pl.BlockSpec(memory_space=pltpu.HBM)],
        out_specs=[vmem] * 3,
        scratch_shapes=[pltpu.VMEM((2, rank, points), jnp.float32), pltpu.SemaphoreType.DMA((2,))],
        compiler_params=pltpu.CompilerParams(vmem_limit_bytes=20 << 20),
        cost_estimate=pl.CostEstimate(flops=400_000_000, bytes_accessed=4 << 20, transcendentals=0),
        name="middle",
    )(current, coeff, pltpu.with_memory_space_constraint(corr, pltpu.HBM))


def final_call(part, near, far, across, coupling, current, last_high, last_low):
    vmem = pl.BlockSpec(memory_space=pltpu.VMEM)
    return pl.pallas_call(
        final_kernel,
        out_shape=jax.ShapeDtypeStruct(current.shape, jnp.float32),
        in_specs=[vmem] * 8,
        out_specs=pl.BlockSpec(memory_space=pltpu.HBM),
        scratch_shapes=[pltpu.VMEM(current.shape, jnp.float32), pltpu.SemaphoreType.DMA((4,))],
        compiler_params=pltpu.CompilerParams(vmem_limit_bytes=12 << 20),
        cost_estimate=pl.CostEstimate(flops=400_000_000, bytes_accessed=4 << 20, transcendentals=0),
        name="final",
    )(part, near, far, across, coupling, current, last_high, last_low)


def local(
    charges, cluster_order, near_tiles, near_index, near_count, proj_basis, corr_basis, coupling
):
    tie = lax.optimization_barrier
    rank = proj_basis.shape[-1]
    other = over_rhs(charges)
    early, second, mid, late, fold = gram_call(corr_basis, proj_basis, coupling)
    early_other = over_rhs(early)
    other, early, second, mid, late, fold = tie((other, early, second, mid, late, fold))
    side = lax.axis_index("rhs").astype(jnp.int32).reshape(1)
    rows = charges.shape[0]
    core = lax.axis_index("core") == 0

    def swapped(value):
        return jnp.concatenate([value[rank:], value[:rank]], axis=0)

    fold = jnp.where(core, fold[0], fold[1]) + swap(jnp.where(core, fold[1], fold[0]), ("core",), 1)
    fold_other = swap(fold, ("x0",), 1)
    current, pair = near_call(
        cluster_order, near_index, near_count, side, charges, other, near_tiles, proj_basis
    )
    pair, early_other, fold_other = tie((pair, early_other, fold_other))
    early = early + early_other
    fold = fold + fold_other
    pair = pair + over_rhs(pair)
    own, sum1 = pair[:rows], pair[rows:]
    later = later_call(current, proj_basis)
    own, later = tie((own, later))
    part2, part3 = later[:rows], later[rows:]

    small = own.shape
    coeff0, own = small_call(
        first_kernel, [small] * 2, own, swap(own, ("core",), 1), sum1, coupling, early)
    own = own + swap(own, ("core",), 1)
    own, fold = tie((own, fold))
    fold = fold + swapped(swap(fold, ("x1", "x0"), 3))
    part2 = part2 - dot(coeff0, second)
    part3 = part3 - dot(coeff0, late[:rank])
    coeff1, own, part3 = small_call(
        second_kernel, [small] * 3, own, swap(own, ("x0",), 1), part2, part3, coupling, mid, late)
    own = own + over_rhs(own)
    both = jnp.concatenate([own, part3], axis=0)
    both = both + swap(both, ("core",), 1)
    both, fold, coeff0, coeff1 = tie((both, fold, coeff0, coeff1))
    fold_other = swap(fold, ("core",), 1)
    fold = jnp.concatenate(
        [jnp.where(core, fold, fold_other), jnp.where(core, fold_other, fold)], axis=1)
    current = current - dot(
        jnp.concatenate([coeff0, coeff1], axis=1), corr_basis[:2].reshape(2 * rank, -1))
    near, far, across = (swap(both, ("x1", "x0"), mask) for mask in (1, 3, 2))
    coeff2, own = small_call(third_kernel, [small] * 2, both, near, far, across, fold, coupling)
    near, far, across = (swap(own, RING, mask) for mask in (1, 17, 16))
    current, last_high, last_low = middle_call(current, coeff2, corr_basis)
    return final_call(own, near, far, across, coupling, current, last_high, last_low)


def solution(mesh):
    split = Mesh(mesh.devices.reshape(-1, 2, 2, 2, 2, 2), AXES)
    every = AXES
    leaf = AXES[:-1]
    return jax.shard_map(
        local,
        mesh=split,
        in_specs=(
            P(None, every),
            P(leaf),
            P(every, None, None, None),
            P(every, None),
            P(every),
            P(None, every, None),
            P(None, None, every),
            P(leaf, None, None, None, None),
        ),
        out_specs=P(None, every),
        check_vma=False,
    )
```

```python
import jax
import jax.numpy as jnp
from jax import lax
from jax.experimental import pallas as pl
from jax.experimental.pallas import tpu as pltpu
from jax.sharding import Mesh, PartitionSpec as P

AXES = ("z", "y", "x1", "x0", "core", "rhs")
FAST = lax.Precision.HIGH


def dot(a, b):
    return jnp.dot(a, b, precision=FAST, preferred_element_type=jnp.float32)


def swap(block, axes, mask):
    count = lax.axis_size(axes)
    return lax.ppermute(block, axes, [(i, i ^ mask) for i in range(count)])


def over_rhs(block):
    return swap(block, ("rhs",), 1)


RING = ("y", "x1", "x0", "core", "rhs")


def mm(a, b):
    return jnp.dot(a, b, preferred_element_type=jnp.float32)

def parts(value):
    high = value.astype(jnp.bfloat16)
    low = (value - high.astype(jnp.float32)).astype(jnp.bfloat16)
    return high, low

def stacked(value):
    high, low = parts(value)
    return jnp.concatenate([high, low], axis=0)

def near_kernel(order, index, count, side, own, other, tiles_hbm, proj_hbm, current, reduced,
                source, gathered, operand, tiles, proj, needed, wanted, tile_sem, proj_sem):
    rows, half = own.shape
    size = tiles.shape[-1]
    slots = index.shape[1]
    leaf_tiles = operand.shape[0]
    out_tiles = tiles.shape[0]
    load_tiles = pltpu.make_async_copy(tiles_hbm, tiles, tile_sem)
    load_tiles.start()
    load_proj = pltpu.make_async_copy(proj_hbm.at[pl.ds(0, 2)], proj, proj_sem)
    load_proj.start()
    own_start = side[0] * half
    other_start = half - own_start
    for block, start in ((own, own_start), (other, other_start)):
        for c in range(half // size):
            at = pl.multiple_of(start + c * size, size)
            source[pl.ds(at, size), :] = block[:, c * size:(c + 1) * size].T

    for tile in range(leaf_tiles):
        needed[tile] = 0
    for t in range(out_tiles):
        for slot in range(slots):
            needed[index[t, jnp.where(slot < count[t], slot, 0)]] = 1

    def note(tile, found):
        wanted[found] = tile
        return found + needed[tile]
    found = lax.fori_loop(0, leaf_tiles, note, 0, unroll=True)
    wanted[found] = wanted[found - 1]

    def fetch(base, slot):
        for u in range(0, size, 8):
            gathered[slot, u:u + 8, :] = jnp.concatenate(
                [source[pl.ds(order[base + u + v], 1), :] for v in range(8)], axis=0)

    fetch(wanted[0] * size, 0)
    def gather(n, _):
        slot = n & 1
        ready = stacked(gathered[slot].T)
        fetch(wanted[n + 1] * size, 1 - slot)
        operand[wanted[n]] = ready
        return 0
    lax.fori_loop(0, found, gather, 0)

    load_tiles.wait()
    def near(t, _):
        pieces = []
        for slot in range(slots):
            live = slot < count[t]
            picked = operand[jnp.where(live, index[t, slot], index[t, 0])]
            pieces.append(jnp.where(live, picked, jnp.zeros_like(picked)))
        left = jnp.concatenate(pieces, axis=1)
        high, low = parts(tiles[t].reshape(slots * size, size))
        both = mm(left, high)
        out = both[:rows] + both[rows:] + mm(left[:rows], low)
        current[:, pl.ds(pl.multiple_of(t * size, size), size)] = out
        return 0
    lax.fori_loop(0, out_tiles, near, 0, unroll=True)
    load_proj.wait()
    left = stacked(current[...])
    for level in range(2):
        high, low = parts(proj[level])
        both = mm(left, high)
        reduced[level * rows:(level + 1) * rows, :] = (
            both[:rows] + both[rows:] + mm(left[:rows], low))

def near_call(order, index, count, side, own, other, tiles, proj):
    rows, half = own.shape
    out_tiles, slots, size, _ = tiles.shape
    rank = proj.shape[-1]
    smem = pl.BlockSpec(memory_space=pltpu.SMEM)
    vmem = pl.BlockSpec(memory_space=pltpu.VMEM)
    hbm = pl.BlockSpec(memory_space=pltpu.HBM)
    return pl.pallas_call(
        near_kernel,
        out_shape=(jax.ShapeDtypeStruct((rows, half), jnp.float32), jax.ShapeDtypeStruct((2 * rows, rank), jnp.float32)),
        in_specs=[smem, smem, smem, smem, vmem, vmem, hbm, hbm],
        out_specs=(vmem, vmem),
        scratch_shapes=[
            pltpu.VMEM((order.shape[0], rows), jnp.float32),
            pltpu.VMEM((2, size, rows), jnp.float32),
            pltpu.VMEM((order.shape[0] // size, 2 * rows, size), jnp.bfloat16),
            pltpu.VMEM(tiles.shape, jnp.float32),
            pltpu.VMEM((2, half, rank), jnp.float32),
            pltpu.SMEM((order.shape[0] // size,), jnp.int32),
            pltpu.SMEM((order.shape[0] // size + 1,), jnp.int32),
            pltpu.SemaphoreType.DMA,
            pltpu.SemaphoreType.DMA,
        ],
        compiler_params=pltpu.CompilerParams(vmem_limit_bytes=24 << 20),
        cost_estimate=pl.CostEstimate(flops=200_000_000, bytes_accessed=8 << 20, transcendentals=0),
        name="near",
    )(order, index, count, side, own, other,
      *(pltpu.with_memory_space_constraint(v, pltpu.HBM) for v in (tiles, proj)))

def later_kernel(current, proj_hbm, reduced, proj, sems):
    rows = current.shape[0]
    loads = [pltpu.make_async_copy(proj_hbm.at[level + 2], proj.at[level], sems.at[level])
             for level in range(2)]
    for load in loads:
        load.start()
    left = stacked(current[...])
    for level in range(2):
        loads[level].wait()
        high, low = parts(proj[level])
        both = mm(left, high)
        reduced[level * rows:(level + 1) * rows, :] = (
            both[:rows] + both[rows:] + mm(left[:rows], low))


def later_call(current, proj):
    rows, points = current.shape
    rank = proj.shape[-1]
    vmem = pl.BlockSpec(memory_space=pltpu.VMEM)
    return pl.pallas_call(
        later_kernel,
        out_shape=jax.ShapeDtypeStruct((2 * rows, rank), jnp.float32),
        in_specs=[vmem, pl.BlockSpec(memory_space=pltpu.HBM)],
        out_specs=vmem,
        scratch_shapes=[pltpu.VMEM((2, points, rank), jnp.float32), pltpu.SemaphoreType.DMA((2,))],
        compiler_params=pltpu.CompilerParams(vmem_limit_bytes=16 << 20),
        cost_estimate=pl.CostEstimate(
            flops=12 * rows * points * rank, bytes_accessed=4 << 20, transcendentals=0),
        name="later",
    )(current, pltpu.with_memory_space_constraint(proj, pltpu.HBM))


def gram_kernel(corr_hbm, proj_hbm, coup_hbm, *rest):
    levels, points, rank = proj_hbm.shape
    early, second, mid, late, fold, corr, proj, coup, sems, coup_sem = rest
    load_coup = pltpu.make_async_copy(coup_hbm.at[0, levels - 2], coup, coup_sem)
    load_coup.start()
    loads = {}
    for level in range(levels - 1):
        loads["c", level] = pltpu.make_async_copy(corr_hbm.at[level], corr.at[level], sems.at[level])
        loads["p", level] = pltpu.make_async_copy(
            proj_hbm.at[level + 1], proj.at[level], sems.at[levels - 1 + level])
        loads["c", level].start()
        loads["p", level].start()
    targets = {(0, 0): (early, 0), (1, 0): (second, 0), (1, 1): (mid, 0),
               (2, 0): (late, 0), (2, 1): (late, 1), (2, 2): (late, 2)}
    lefts = []
    for above in range(levels - 1):
        loads["c", above].wait()
        left_high, left_low = parts(corr[above])
        lefts.append((left_high, left_low))
        loads["p", above].wait()
        high, low = parts(proj[above])
        for below in range(above + 1):
            left_high, left_low = lefts[below]
            target, place = targets[above, below]
            target[place * rank:(place + 1) * rank, :] = (
                mm(left_high, high) + mm(left_high, low) + mm(left_low, high))
    load_coup.wait()
    left_high, left_low = parts(coup[...].reshape(2 * rank, rank))
    high, low = parts(late[2 * rank:3 * rank, :])
    out = mm(left_high, high) + mm(left_high, low) + mm(left_low, high)
    for part in range(2):
        fold[part] = out[:, part * rank // 2:(part + 1) * rank // 2]


def gram_call(corr, proj, coup):
    levels, points, rank = proj.shape
    pairs = levels * (levels - 1) // 2
    hbm = pl.BlockSpec(memory_space=pltpu.HBM)
    vmem = pl.BlockSpec(memory_space=pltpu.VMEM)
    return pl.pallas_call(
        gram_kernel,
        out_shape=[jax.ShapeDtypeStruct((above * rank, rank), jnp.float32) for above in (1, 1, 1, 3)]
        + [jax.ShapeDtypeStruct((2, 2 * rank, rank // 2), jnp.float32)],
        in_specs=[hbm, hbm, hbm],
        out_specs=[vmem] * (levels + 1),
        scratch_shapes=[
            pltpu.VMEM((levels - 1, rank, points), jnp.float32),
            pltpu.VMEM((levels - 1, points, rank), jnp.float32),
            pltpu.VMEM((2, rank, rank), jnp.float32),
            pltpu.SemaphoreType.DMA((2 * levels - 2,)),
            pltpu.SemaphoreType.DMA,
        ],
        compiler_params=pltpu.CompilerParams(vmem_limit_bytes=32 << 20),
        cost_estimate=pl.CostEstimate(
            flops=6 * pairs * points * rank * rank, bytes_accessed=12 << 20, transcendentals=0),
        name="gram",
    )(*(pltpu.with_memory_space_constraint(v, pltpu.HBM) for v in (corr, proj, coup)))


def apply(value, matrix):
    rows = value.shape[0]
    left = stacked(value)
    high, low = parts(matrix)
    both = mm(left, high)
    return both[:rows] + both[rows:] + mm(left[:rows], low)


def level_coefficients(height, own, sib, coupling):
    rank = own.shape[1]
    pair = jnp.concatenate([own, sib], axis=1)
    return apply(pair, coupling[0, height].reshape(2 * rank, rank))


def first_kernel(own, sib, total, coupling, gram, coeff, after):
    value = level_coefficients(0, own[...], sib[...], coupling)
    coeff[...] = value
    after[...] = total[...] - apply(value, gram[...])


def second_kernel(own, sib, part2, part3, coupling, gram2, gram3, coeff, after2, after3):
    rank = own.shape[1]
    value = level_coefficients(1, own[...], sib[...], coupling)
    coeff[...] = value
    after2[...] = part2[...] - apply(value, gram2[...])
    after3[...] = part3[...] - apply(value, gram3[rank:2 * rank, :])


def third_kernel(both, near, far, across, fold, coupling, coeff, after):
    rows, rank = coeff.shape
    mine = both[...] + near[...]
    others = far[...] + across[...]
    own, sib = mine[:rows], others[:rows]
    coeff[...] = level_coefficients(2, own, sib, coupling)
    after[...] = (mine[rows:] + others[rows:]) - apply(
        jnp.concatenate([own, sib], axis=1), fold[...])


def middle_kernel(current, coeff, corr_hbm, after, last_high, last_low, corr, sems):
    loads = [pltpu.make_async_copy(corr_hbm.at[level + 2], corr.at[level], sems.at[level])
             for level in range(2)]
    for load in loads:
        load.start()
    loads[0].wait()
    after[...] = current[...] - apply(coeff[...], corr[0])
    loads[1].wait()
    last_high[...], last_low[...] = parts(corr[1])


def final_kernel(part, near, far, across, coupling, current, last_high, last_low, out_hbm, out, sems):
    rows, points = current.shape
    coeff = level_coefficients(3, part[...] + near[...], far[...] + across[...], coupling)
    left = stacked(coeff)
    step = points // 2
    copies = []
    for piece in range(2):
        cols = slice(piece * step, (piece + 1) * step)
        value = mm(left, last_high[:, cols])
        out[:, cols] = current[:, cols] - (
            value[:rows] + value[rows:] + mm(left[:rows], last_low[:, cols]))
        copies.append(pltpu.make_async_copy(out.at[:, cols], out_hbm.at[:, cols], sems.at[piece]))
        copies[-1].start()
    for copy in copies:
        copy.wait()


def small_call(kernel, shapes, *args):
    vmem = pl.BlockSpec(memory_space=pltpu.VMEM)
    return pl.pallas_call(
        kernel,
        out_shape=[jax.ShapeDtypeStruct(shape, jnp.float32) for shape in shapes],
        in_specs=[vmem] * len(args),
        out_specs=[vmem] * len(shapes),
        compiler_params=pltpu.CompilerParams(vmem_limit_bytes=8 << 20),
        cost_estimate=pl.CostEstimate(flops=100_000_000, bytes_accessed=1 << 20, transcendentals=0),
    )(*args)


def middle_call(current, coeff, corr):
    rank, points = corr.shape[1:]
    vmem = pl.BlockSpec(memory_space=pltpu.VMEM)
    half = jax.ShapeDtypeStruct((rank, points), jnp.bfloat16)
    return pl.pallas_call(
        middle_kernel,
        out_shape=[jax.ShapeDtypeStruct(current.shape, jnp.float32), half, half],
        in_specs=[vmem, vmem, pl.BlockSpec(memory_space=pltpu.HBM)],
        out_specs=[vmem] * 3,
        scratch_shapes=[pltpu.VMEM((2, rank, points), jnp.float32), pltpu.SemaphoreType.DMA((2,))],
        compiler_params=pltpu.CompilerParams(vmem_limit_bytes=20 << 20),
        cost_estimate=pl.CostEstimate(flops=400_000_000, bytes_accessed=4 << 20, transcendentals=0),
        name="middle",
    )(current, coeff, pltpu.with_memory_space_constraint(corr, pltpu.HBM))


def final_call(part, near, far, across, coupling, current, last_high, last_low):
    vmem = pl.BlockSpec(memory_space=pltpu.VMEM)
    return pl.pallas_call(
        final_kernel,
        out_shape=jax.ShapeDtypeStruct(current.shape, jnp.float32),
        in_specs=[vmem] * 8,
        out_specs=pl.BlockSpec(memory_space=pltpu.HBM),
        scratch_shapes=[pltpu.VMEM(current.shape, jnp.float32), pltpu.SemaphoreType.DMA((2,))],
        compiler_params=pltpu.CompilerParams(vmem_limit_bytes=12 << 20),
        cost_estimate=pl.CostEstimate(flops=400_000_000, bytes_accessed=4 << 20, transcendentals=0),
        name="final",
    )(part, near, far, across, coupling, current, last_high, last_low)


def local(
    charges, cluster_order, near_tiles, near_index, near_count, proj_basis, corr_basis, coupling
):
    tie = lax.optimization_barrier
    rank = proj_basis.shape[-1]
    other = over_rhs(charges)
    early, second, mid, late, fold = gram_call(corr_basis, proj_basis, coupling)
    early_other = over_rhs(early)
    other, early, second, mid, late, fold = tie((other, early, second, mid, late, fold))
    side = lax.axis_index("rhs").astype(jnp.int32).reshape(1)
    rows = charges.shape[0]
    core = lax.axis_index("core") == 0

    def swapped(value):
        return jnp.concatenate([value[rank:], value[:rank]], axis=0)

    fold = jnp.where(core, fold[0], fold[1]) + swap(jnp.where(core, fold[1], fold[0]), ("core",), 1)
    fold_other = swap(fold, ("x0",), 1)
    current, pair = near_call(
        cluster_order, near_index, near_count, side, charges, other, near_tiles, proj_basis
    )
    pair, early_other, fold_other = tie((pair, early_other, fold_other))
    early = early + early_other
    fold = fold + fold_other
    pair = pair + over_rhs(pair)
    own, sum1 = pair[:rows], pair[rows:]
    later = later_call(current, proj_basis)
    own, later = tie((own, later))
    part2, part3 = later[:rows], later[rows:]

    small = own.shape
    coeff0, own = small_call(
        first_kernel, [small] * 2, own, swap(own, ("core",), 1), sum1, coupling, early)
    own = own + swap(own, ("core",), 1)
    own, fold = tie((own, fold))
    fold = fold + swapped(swap(fold, ("x1", "x0"), 3))
    part2 = part2 - dot(coeff0, second)
    part3 = part3 - dot(coeff0, late[:rank])
    coeff1, own, part3 = small_call(
        second_kernel, [small] * 3, own, swap(own, ("x0",), 1), part2, part3, coupling, mid, late)
    own = own + over_rhs(own)
    both = jnp.concatenate([own, part3], axis=0)
    both = both + swap(both, ("core",), 1)
    both, fold, coeff0, coeff1 = tie((both, fold, coeff0, coeff1))
    fold_other = swap(fold, ("core",), 1)
    fold = jnp.concatenate(
        [jnp.where(core, fold, fold_other), jnp.where(core, fold_other, fold)], axis=1)
    current = current - dot(
        jnp.concatenate([coeff0, coeff1], axis=1), corr_basis[:2].reshape(2 * rank, -1))
    near, far, across = (swap(both, ("x1", "x0"), mask) for mask in (1, 3, 2))
    coeff2, own = small_call(third_kernel, [small] * 2, both, near, far, across, fold, coupling)
    near, far, across = (swap(own, RING, mask) for mask in (1, 17, 16))
    current, last_high, last_low = middle_call(current, coeff2, corr_basis)
    return final_call(own, near, far, across, coupling, current, last_high, last_low)


def solution(mesh):
    split = Mesh(mesh.devices.reshape(-1, 2, 2, 2, 2, 2), AXES)
    every = AXES
    leaf = AXES[:-1]
    return jax.shard_map(
        local,
        mesh=split,
        in_specs=(
            P(None, every),
            P(leaf),
            P(every, None, None, None),
            P(every, None),
            P(every),
            P(None, every, None),
            P(None, None, every),
            P(leaf, None, None, None, None),
        ),
        out_specs=P(None, every),
        check_vma=False,
    )
```
